256 devices in a mesh: seg: 64 (over y, z, core), head: 4 (over x).
Axes of the slice: x: 4, y: 4, z: 8, core: 2. Of those that a mesh axis runs over, the one named last changes fastest.
Arguments:
- queries: bfloat16 [16384, 2048], P('seg', 'head'), may hold values from -20 to 20
- keys: bfloat16 [16384, 2048], P('seg', 'head'), may hold values from -12 to 12
- values: bfloat16 [16384, 2048], P('seg', 'head'), may hold values from -6 to 6
- out_grad: bfloat16 [16384, 2048], P('seg', 'head'), may hold values from -5 to 5
- out_weight: bfloat16 [2048, 2048], P('head'), may hold values from -1 to 1
- retr_owner: int32 [64, 32], replicated, may hold values from 0 to 63, as said below
- retr_block: int32 [64, 32], replicated, may hold values from -1 to 1, as said below
Outputs:
- layer_out: bfloat16 [16384, 2048], P('seg', 'head')
- query_grad: bfloat16 [16384, 2048], P('seg', 'head')
- key_grad: bfloat16 [16384, 2048], P('seg', 'head')
- value_grad: bfloat16 [16384, 2048], P('seg', 'head')
- proj_grad_t: float32 [2048, 2048], P('seg', 'head')
The draws below stay inside these ranges and needn't reach their ends.
Inputs may be any that keep to these rules, and one draw needn't show every extreme that they name: `retr_owner`: row s lists 32 owners, all different from one another and from s. `retr_block`: padding (-1) comes after the live entries of a row; every row has at least 24 live entries.
All inputs are finite; a program needn't handle non-finite values.
Results may differ from the reference program's by a relative error of at most 0.012.
Values may be sent and summed in bfloat16 or wider, within the bound.
A program may use at most 128 MiB of HBM per device.

```python
import math
import jax
import jax.numpy as jnp
from jax import lax

D = 2048
HEADS = 16
DH = 128
BLOCK = 128
SEG = 256
SEGMENTS = 64
TOKENS = 16384
MEMB = 2
R = 32


def draw_queries(key, part):
    spread = 2.0 * jnp.clip(jax.random.normal(jax.random.fold_in(key, 1), (TOKENS, HEADS * DH), jnp.float32), -6.0, 6.0)
    return spread.astype(jnp.bfloat16)


def draw_keys(key, part):
    spread = jnp.clip(jax.random.normal(jax.random.fold_in(key, 2), (TOKENS, HEADS * DH), jnp.float32), -6.0, 6.0)
    return spread.astype(jnp.bfloat16)


def draw_retr_owner(key, part):
    streams = jax.random.split(jax.random.fold_in(key, 5), SEGMENTS)
    orders = jax.vmap(lambda stream: jax.random.permutation(stream, SEGMENTS - 1))(streams)[:, :R]
    return ((jnp.arange(SEGMENTS)[:, None] + 1 + orders) % SEGMENTS).astype(jnp.int32)


def draw_retr_block(key, part):
    first_key, second_key = jax.random.split(jax.random.fold_in(key, 7))
    blocks = jax.random.randint(first_key, (SEGMENTS, R), 0, MEMB)
    blocks = blocks.at[0, 0].set(MEMB - 1)
    live_count = jax.random.randint(second_key, (SEGMENTS,), R - R // 4, R + 1)
    live_count = live_count.at[0].set(R).at[1].set(R - R // 4)
    places = jnp.arange(R)
    return jnp.where(places[None, :] < live_count[:, None], blocks, -1).astype(jnp.int32)


def spiked(array, key, source, target, shards_of, factor):
    def block_of(dim):
        return (jnp.arange(array.shape[dim]) // (array.shape[dim] // shards_of)).reshape((-1,) + (1,) * (array.ndim - 1 - dim))

    first = jax.random.permutation(key, shards_of)[block_of(target)]
    far = (block_of(target) + shards_of // 2) % shards_of
    return jnp.where((block_of(source) == first) | (block_of(source) == far), factor * array, array)


def block_scale(key, shape, cuts, low, high):
    gain = 1.0
    for axis_at, parts in cuts:
        heights = jax.random.uniform(jax.random.fold_in(jax.random.fold_in(key, 6), axis_at), (parts,), jnp.float32, low / len(cuts), high / len(cuts))
        gain = gain * jnp.repeat(jnp.exp(heights), shape[axis_at] // parts).reshape((-1,) + (1,) * (len(shape) - 1 - axis_at))
    return gain


def scatter_about(rng, shape, deviation, bound, pieces=(), kind=jnp.bfloat16):
    entries = jax.random.normal(rng, shape, jnp.float32) * deviation
    if len(pieces) > 0:
        entries = block_scale(rng, shape, pieces, -0.22, 0.18) * entries
    return jnp.clip(entries, min=-bound, max=bound).astype(kind)


def gaussian_with(stream_key, extent, scale, bound, cuts, heavy, held_as=jnp.bfloat16):
    values = scale * jax.random.normal(stream_key, extent, jnp.float32)
    if cuts:
        values = values * block_scale(stream_key, extent, cuts, -0.22, 0.18)
    return jnp.clip(spiked(values, jax.random.fold_in(stream_key, 3), *heavy), -bound, bound).astype(held_as)


def setup_inputs(seed: int = 0) -> dict:
    splits = jax.random.split(jax.random.key(seed), 8)
    return {
        "queries": draw_queries(jax.random.fold_in(splits[7], 71), 0),
        "keys": draw_keys(jax.random.fold_in(splits[7], 71), 0),
        "values": scatter_about(splits[2], (TOKENS, HEADS * DH), 1.0, 6.0, ((0, 64), (1, 4))),
        "out_grad": gaussian_with(splits[3], (TOKENS, D), 0.125, 5.0, ((0, 64), (1, 4)), (0, 1, 64, 4.0)),
        "out_weight": scatter_about(splits[4], (HEADS * DH, D), (DH // 4) ** -0.5, 1.0, ((0, 4),)),
        "retr_owner": draw_retr_owner(jax.random.fold_in(splits[7], 71), 0),
        "retr_block": draw_retr_block(jax.random.fold_in(splits[7], 71), 0),
    }


def split_heads(tok_rows, count):
    return tok_rows.reshape(tok_rows.shape[0], count, -1).transpose(1, 0, 2)

def join_heads(stacked):
    return stacked.transpose(1, 0, 2).reshape(stacked.shape[1], -1)

def product(form, left_side, right_side):
    return jnp.einsum(form, left_side.astype(jnp.float32), right_side.astype(jnp.float32))

def attend(queries, keys, values, cache_k, cache_v, mem_k, mem_v, mem_live, has_cache, d_attn, score_scale):
    length = queries.shape[1]
    causal = jnp.arange(length)[:, None] >= jnp.arange(length)[None, :]
    own = jnp.where(causal[None], product('hqd,hkd->hqk', queries, keys) * score_scale, -jnp.inf)
    cached = jnp.where(has_cache, product('hqd,hkd->hqk', queries, cache_k) * score_scale, -jnp.inf)
    stored = jnp.where(mem_live[None, None, :], product('hqd,hkd->hqk', queries, mem_k) * score_scale, -jnp.inf)
    row_top = jnp.maximum(jnp.maximum(lax.optimization_barrier(jnp.max(own, -1)), lax.optimization_barrier(jnp.max(cached, -1))), lax.optimization_barrier(jnp.max(stored, -1)))[..., None]
    row_total = lax.optimization_barrier(jnp.sum(jnp.exp(own - row_top), -1)) + lax.optimization_barrier(jnp.sum(jnp.exp(cached - row_top), -1)) + lax.optimization_barrier(jnp.sum(jnp.exp(stored - row_top), -1))
    log_total = row_top + jnp.log(row_total)[..., None]
    weights = [jnp.exp(group_scores - log_total) for group_scores in (own, cached, stored)]
    rounded = [entry.astype(jnp.bfloat16) for entry in weights]
    sources = (values, cache_v, mem_v)
    mixed_sum = product('hqk,hkd->hqd', rounded[0], sources[0]) + product('hqk,hkd->hqd', rounded[1], sources[1]) + product('hqk,hkd->hqd', rounded[2], sources[2])
    attn = mixed_sum.astype(jnp.bfloat16)
    row_delta = lax.optimization_barrier(jnp.sum(d_attn.astype(jnp.float32) * attn.astype(jnp.float32), -1))[..., None]
    slopes = [(entry * (product('hqd,hkd->hqk', d_attn, source) - row_delta)).astype(jnp.bfloat16) for entry, source in zip(weights, sources)]
    grad_q = score_scale * (product('hqk,hkd->hqd', slopes[0], keys) + product('hqk,hkd->hqd', slopes[1], cache_k) + product('hqk,hkd->hqd', slopes[2], mem_k))
    grad_k_own = score_scale * product('hqk,hqd->hkd', slopes[0], queries)
    grad_v_own = product('hqk,hqd->hkd', rounded[0], d_attn)
    grad_k_cache = score_scale * product('hqk,hqd->hkd', slopes[1], queries)
    grad_v_cache = product('hqk,hqd->hkd', rounded[1], d_attn)
    return (attn, grad_q, grad_k_own, grad_v_own, grad_k_cache, grad_v_cache)

def reference(queries, keys, values, out_grad, out_weight, retr_owner, retr_block):
    score_scale = 1.0 / math.sqrt(DH)
    d_attn = jnp.dot(out_grad, out_weight.T, preferred_element_type=jnp.float32).astype(jnp.bfloat16)
    offsets = jnp.arange(BLOCK, dtype=jnp.int32)

    def one_segment(segment):

        def rows_at(source, begin):
            return split_heads(lax.dynamic_slice_in_dim(source, begin, SEG, 0), HEADS)
        start = (segment * SEG).astype(jnp.int32)
        previous = (jnp.maximum(segment - 1, 0) * SEG).astype(jnp.int32)
        owners = retr_owner[segment]
        blocks = retr_block[segment]
        picked = ((owners * SEG + jnp.maximum(blocks, 0) * BLOCK)[:, None] + offsets[None, :]).reshape(-1).astype(jnp.int32)
        mem_k = split_heads(keys[picked], HEADS)
        mem_v = split_heads(values[picked], HEADS)
        mem_live = jnp.repeat(blocks >= 0, BLOCK)
        results = attend(rows_at(queries, start), rows_at(keys, start), rows_at(values, start), rows_at(keys, previous), rows_at(values, previous), mem_k, mem_v, mem_live, segment > 0, rows_at(d_attn, start), score_scale)
        return tuple((join_heads(entry) for entry in results))
    attn, grad_q, grad_k_own, grad_v_own, grad_k_cache, grad_v_cache = lax.map(one_segment, jnp.arange(SEGMENTS, dtype=jnp.int32))
    carried_k = jnp.concatenate([grad_k_cache[1:], jnp.zeros_like(grad_k_cache[:1])], 0)
    carried_v = jnp.concatenate([grad_v_cache[1:], jnp.zeros_like(grad_v_cache[:1])], 0)
    attn_rows = attn.reshape(TOKENS, -1)
    layer_out = jnp.dot(attn_rows, out_weight, preferred_element_type=jnp.float32).astype(jnp.bfloat16)
    query_grad = grad_q.reshape(TOKENS, -1).astype(jnp.bfloat16)
    key_grad = (grad_k_own + carried_k).reshape(TOKENS, -1).astype(jnp.bfloat16)
    value_grad = (grad_v_own + carried_v).reshape(TOKENS, -1).astype(jnp.bfloat16)
    proj_grad_t = jnp.dot(out_grad.T, attn_rows, preferred_element_type=jnp.float32)
    return (layer_out, query_grad, key_grad, value_grad, proj_grad_t)
```

```python
import functools
import math

import jax
import jax.numpy as jnp
from jax import lax
from jax.experimental import pallas as pl
from jax.experimental.pallas import tpu as pltpu
from jax.sharding import PartitionSpec as P

DH = 128
NY, NZ, NX = 4, 8, 4
HD = 4
R = 32
SPLIT = 48
STAGGER = 4
LOG2E = 1.4426950408889634
F32 = jnp.float32
BF16 = jnp.bfloat16
MESH = pl.DeviceIdType.MESH


def mm(a, b, ca, cb):
    return lax.dot_general(a, b, (((ca,), (cb,)), ((), ())), preferred_element_type=F32)


def body(
    q_ref, k_ref, v_ref, og_ref, w_ref, owner_ref, block_ref,
    lo_ref, qg_ref, kg_ref, vg_ref, pg_ref,
    kv0, kv1, kv2, kv3,
    s_ref, stat_a, stat_b, acc_ref,
    og_all, og_t, w_col, da_ref, at_own, at_all,
    pj_f, pj_b, pp_recv, py_send, py_own, py_recv, pz_send, pz_own, pz_recv,
    cg_send, cg_recv, own_kv,
    loc_sem, bz_s, bz_r, az_s, az_r, ay_s, ay_r, b1_s, b1_r, b2_s, b2_r,
    pa_s, pa_r, pb_s, pb_r, ogx_s, ogx_r, wx_s, wx_r, at_s, at_r,
    pp_s, pp_r, py_s, py_r, pz_s, pz_r, cg_s, cg_r,
):
    kvs = (kv0, kv1, kv2, kv3)
    seg = lax.axis_index("seg")
    x = lax.axis_index("head")
    c = seg % 2
    z = (seg // 2) % NZ
    y = seg // (2 * NZ)
    scale = 1.0 / math.sqrt(DH)

    def sid(yy, zz, cc):
        return (yy * NZ + zz) * 2 + cc

    def zat(d):
        return (z + d + NZ) % NZ

    def yat(d):
        return (y + d + NY) % NY

    def xat(d):
        return (x + d + NX) % NX

    def at_seg(s):
        return {"seg": s, "head": x}

    zdev = {d: at_seg(sid(y, zat(d), c)) for d in (-3, -2, -1, 1, 2, 3, 4)}
    ydev = {d: at_seg(sid(yat(d), z, c)) for d in (-1, 1, 2)}
    xdev = {d: {"seg": seg, "head": xat(d)} for d in (-1, 1, 2)}
    partner = at_seg(sid(y, z, 1 - c))
    before = at_seg((seg + 63) % 64)
    after = at_seg((seg + 1) % 64)

    local = []
    for h in range(HD):
        cols = pl.ds(h * DH, DH)
        for i, ref in enumerate((k_ref, v_ref)):
            for b in range(2):
                cp = pltpu.make_async_copy(
                    ref.at[pl.ds(b * 128, 128), cols],
                    kvs[h].at[y, z, c, 2 * i + b],
                    loc_sem.at[h, 2 * i + b],
                )
                cp.start()
                local.append(cp)
    og_local = pltpu.make_async_copy(og_ref, og_all.at[x], loc_sem.at[4, 0])
    og_local.start()
    w_local = pltpu.make_async_copy(
        w_ref.at[:, pl.ds(pl.multiple_of(x * 512, 512), 512)], w_col.at[x], loc_sem.at[4, 1]
    )
    w_local.start()

    barrier = pltpu.get_barrier_semaphore()
    peers = list(zdev.values()) + list(ydev.values()) + list(xdev.values()) + [partner, before, after]
    for dev in peers:
        pl.semaphore_signal(barrier, inc=1, device_id=dev, device_id_type=MESH)
    pl.semaphore_wait(barrier, len(peers))

    sent = []

    def send(src, dst, ssem, rsem, dev):
        cp = pltpu.make_async_remote_copy(
            src_ref=src, dst_ref=dst, send_sem=ssem, recv_sem=rsem, device_id=dev, device_id_type=MESH
        )
        cp.start()
        sent.append(cp)

    def arrived(dst, ssem, rsem, dev):
        pltpu.make_async_remote_copy(
            src_ref=dst, dst_ref=dst, send_sem=ssem, recv_sem=rsem, device_id=dev, device_id_type=MESH
        ).wait_recv()

    rows_a = pl.ds(0, SPLIT)
    rows_b = pl.ds(SPLIT, 128 - SPLIT)
    everything = pl.ds(0, 4)
    half_k = pl.ds(0, 2)
    half_v = pl.ds(2, 2)

    def part_a(h, yy, zz, which=everything):
        return kvs[h].at[yy, zz, c, which, rows_a]

    def part_b(h, yy, zz, which=everything):
        return kvs[h].at[yy, zz, c, which, rows_b]

    def group_a(h, zz, which=everything):
        return kvs[h].at[:, zz, c, which, rows_a]

    def bz_send(h, hop):
        for d, sign in ((0, 1), (1, -1)):
            which = everything if hop < 4 else (half_k, half_v)[d]
            ref = part_b(h, y, zat(-sign * (hop - 1)), which)
            send(ref, ref, bz_s.at[h, d, hop - 1], bz_r.at[h, d, hop - 1], zdev[sign])

    def bz_wait(h, hop):
        for d, sign in ((0, 1), (1, -1)):
            which = everything if hop < 4 else (half_k, half_v)[d]
            ref = part_b(h, y, zat(-sign * hop), which)
            arrived(ref, bz_s.at[h, d, hop - 1], bz_r.at[h, d, hop - 1], zdev[sign])

    def b1_send(h, dz):
        for d, sign in ((0, 1), (1, -1)):
            ref = part_b(h, y, zat(dz))
            send(ref, ref, b1_s.at[h, d, dz % 8], b1_r.at[h, d, dz % 8], ydev[sign])

    def b1_wait(h, dz):
        for d, sign in ((0, 1), (1, -1)):
            ref = part_b(h, yat(-sign), zat(dz))
            arrived(ref, b1_s.at[h, d, dz % 8], b1_r.at[h, d, dz % 8], ydev[sign])

    def turn(dz):
        return 1 if (dz % 8) in (0, 1, 3, 6) else -1

    def b2_send(h, dz):
        ref = part_b(h, yat(-turn(dz)), zat(dz))
        send(ref, ref, b2_s.at[h, dz % 8], b2_r.at[h, dz % 8], ydev[turn(dz)])

    def b2_wait(h, dz):
        ref = part_b(h, yat(2), zat(dz))
        arrived(ref, b2_s.at[h, dz % 8], b2_r.at[h, dz % 8], ydev[turn(dz)])

    def ay_send(h, hop):
        for d, sign in ((0, 1), (1, -1)):
            which = everything if hop < 2 else (half_k, half_v)[d]
            ref = part_a(h, yat(-sign * (hop - 1)), z, which)
            send(ref, ref, ay_s.at[h, d, hop - 1], ay_r.at[h, d, hop - 1], ydev[sign])

    def ay_wait(h, hop):
        for d, sign in ((0, 1), (1, -1)):
            which = everything if hop < 2 else (half_k, half_v)[d]
            ref = part_a(h, yat(-sign * hop), z, which)
            arrived(ref, ay_s.at[h, d, hop - 1], ay_r.at[h, d, hop - 1], ydev[sign])

    def az_send(h, hop):
        for d, sign in ((0, 1), (1, -1)):
            which = everything if hop < 4 else (half_k, half_v)[d]
            ref = group_a(h, zat(-sign * (hop - 1)), which)
            send(ref, ref, az_s.at[h, d, hop - 1], az_r.at[h, d, hop - 1], zdev[sign])

    def az_wait(h, hop):
        for d, sign in ((0, 1), (1, -1)):
            which = everything if hop < 4 else (half_k, half_v)[d]
            ref = group_a(h, zat(-sign * hop), which)
            arrived(ref, az_s.at[h, d, hop - 1], az_r.at[h, d, hop - 1], zdev[sign])

    def pa_send(h, dz):
        ref = group_a(h, zat(dz))
        send(ref, ref, pa_s.at[h, dz % 8], pa_r.at[h, dz % 8], partner)

    def pb_send(h, dz):
        ref = kvs[h].at[:, zat(dz), c, :, rows_b]
        send(ref, ref, pb_s.at[h, dz % 8], pb_r.at[h, dz % 8], partner)

    def partner_wait(h):
        for dz in range(8):
            ref = kvs[h].at[:, zat(dz), 1 - c, :, rows_a]
            arrived(ref, pa_s.at[h, dz], pa_r.at[h, dz], partner)
            ref = kvs[h].at[:, zat(dz), 1 - c, :, rows_b]
            arrived(ref, pb_s.at[h, dz], pb_r.at[h, dz], partner)

    def tick(h, r):
        if r == 0:
            for cp in local[4 * h : 4 * h + 4]:
                cp.wait()
            bz_send(h, 1)
            ay_send(h, 1)
            b1_send(h, 0)
        elif r == 1:
            bz_wait(h, 1)
            bz_send(h, 2)
            ay_wait(h, 1)
            ay_send(h, 2)
            b1_send(h, 1)
            b1_send(h, -1)
            b1_wait(h, 0)
            b2_send(h, 0)
        elif r == 2:
            bz_wait(h, 2)
            bz_send(h, 3)
            ay_wait(h, 2)
            az_send(h, 1)
            pa_send(h, 0)
            b1_send(h, 2)
            b1_send(h, -2)
            for dz in (1, -1):
                b1_wait(h, dz)
                b2_send(h, dz)
            b2_wait(h, 0)
            pb_send(h, 0)
        elif r in (3, 4, 5):
            n = r - 2
            if r == 3:
                bz_wait(h, 3)
                bz_send(h, 4)
            if r == 4:
                bz_wait(h, 4)
            az_wait(h, n)
            az_send(h, n + 1)
            pa_send(h, n)
            pa_send(h, -n)
            if r == 3:
                b1_send(h, 3)
                b1_send(h, -3)
            if r == 4:
                b1_send(h, 4)
            for dz in (n + 1, -n - 1) if r < 5 else (4,):
                b1_wait(h, dz)
                b2_send(h, dz)
            for dz in (n, -n):
                b2_wait(h, dz)
                pb_send(h, dz)
        elif r == 6:
            az_wait(h, 4)
            pa_send(h, 4)
            b2_wait(h, 4)
            pb_send(h, 4)
        elif r == 7:
            partner_wait(h)

    def slot_ticks(t):
        for h in range(HD):
            if 0 <= t - STAGGER * h <= 7:
                tick(h, t - STAGGER * h)

    def x_sends():
        for d in (1, -1, 2):
            send(og_ref, og_all.at[x], ogx_s.at[d % 4], ogx_r.at[d % 4], xdev[d])
        for d in (1, -1, 2):
            src = w_ref.at[:, pl.ds(pl.multiple_of(xat(d) * 512, 512), 512)]
            send(src, w_col.at[x], wx_s.at[d % 4], wx_r.at[d % 4], xdev[d])

    def og_wait():
        og_local.wait()
        for d in (1, -1, 2):
            arrived(og_all.at[xat(-d)], ogx_s.at[d % 4], ogx_r.at[d % 4], xdev[d])

    def w_wait():
        w_local.wait()
        for d in (1, -1, 2):
            arrived(w_col.at[xat(-d)], wx_s.at[d % 4], wx_r.at[d % 4], xdev[d])

    def make_da():
        total = jnp.zeros((256, 512), F32)
        for i in range(NX):
            total = total + mm(og_all[i], w_ref[:, i * 512 : (i + 1) * 512], 1, 1)
        for h in range(HD):
            da_ref[h] = total[:, h * DH : (h + 1) * DH].astype(BF16)
        for i in range(NX):
            og_t[i] = og_all[i].T

    def entry(kv, j, kind):
        owner = owner_ref[seg, j]
        block = jnp.maximum(block_ref[seg, j], 0)
        return kv[owner // 16, (owner // 2) % 8, owner % 2, kind * 2 + block]

    def pair(kv, j, kind):
        return jnp.concatenate([entry(kv, j, kind), entry(kv, j + 1, kind)], 0)

    def bias(j):
        return jnp.where(block_ref[seg, j] >= 0, 0.0, -jnp.inf).astype(F32)

    prev_seg = (seg + 63) % 64

    def load_own(h):
        for kind in range(2):
            for b in range(2):
                rows = pl.ds(b * 128, 128)
                own_kv[kind, rows] = kvs[h][prev_seg // 16, (prev_seg // 2) % 8, prev_seg % 2, kind * 2 + b]
                own_kv[2 + kind, rows] = kvs[h][y, z, c, kind * 2 + b]

    def q_of(h):
        return q_ref[:, h * DH : (h + 1) * DH]

    def p1_own(h):
        load_own(h)
        q = q_of(h)
        factor = scale * LOG2E
        no_cache = jnp.where(seg > 0, 0.0, -jnp.inf).astype(F32)
        sc = mm(q, own_kv[0], 1, 1) * factor + no_cache
        so = mm(q, own_kv[2], 1, 1) * factor
        keep = lax.broadcasted_iota(jnp.int32, (256, 256), 0) >= lax.broadcasted_iota(jnp.int32, (256, 256), 1)
        so = jnp.where(keep, so, -jnp.inf)
        s_ref[32] = sc[:, :128]
        s_ref[33] = sc[:, 128:]
        s_ref[34] = so[:, :128]
        s_ref[35] = so[:, 128:]
        stat_a[...] = jnp.maximum(
            jnp.maximum(sc[:, :128], sc[:, 128:]), jnp.maximum(so[:, :128], so[:, 128:])
        )

    def p1(h, lo, hi):
        factor = scale * LOG2E

        def step(i, carry):
            j = i * 2
            s = mm(q_of(h), pair(kvs[h], j, 0), 1, 1) * factor
            s0 = s[:, :128] + bias(j)
            s1 = s[:, 128:] + bias(j + 1)
            s_ref[j] = s0
            s_ref[j + 1] = s1
            stat_a[...] = jnp.maximum(stat_a[...], jnp.maximum(s0, s1))
            return carry

        lax.fori_loop(lo, hi, step, 0)

    def p2_pair(j, v):
        p0 = jnp.exp2(s_ref[j] - stat_a[...])
        p1_ = jnp.exp2(s_ref[j + 1] - stat_a[...])
        s_ref[j] = p0
        s_ref[j + 1] = p1_
        stat_b[...] += p0 + p1_
        pb = jnp.concatenate([p0, p1_], 1).astype(BF16)
        acc_ref[...] += mm(pb, v, 1, 0)

    def p2_own(h):
        stat_a[...] = jnp.broadcast_to(jnp.max(stat_a[...], -1, keepdims=True), (256, 128))
        stat_b[...] = jnp.zeros((256, 128), F32)
        acc_ref[...] = jnp.zeros((256, 128), F32)
        p2_pair(32, own_kv[1])
        p2_pair(34, own_kv[3])

    def p2(h, lo, hi):
        def step(i, carry):
            p2_pair(i * 2, pair(kvs[h], i * 2, 1))
            return carry

        lax.fori_loop(lo, hi, step, 0)

    def finish_fwd(h):
        inv = 1.0 / jnp.sum(stat_b[...], -1, keepdims=True)
        attn = (acc_ref[...] * inv).astype(BF16)
        at_own[h] = attn
        da = da_ref[h].astype(F32)
        delta = jnp.sum(da * attn.astype(F32), -1, keepdims=True)
        stat_a[...] = jnp.broadcast_to(inv, (256, 128))
        stat_b[...] = jnp.broadcast_to(delta, (256, 128))
        for d in (1, -1, 2):
            send(at_own.at[h], at_all.at[x, h], at_s.at[h, d % 4], at_r.at[h, d % 4], xdev[d])

    def proj(h):
        for i in range(NX):
            part = mm(og_t[i], at_own[h], 1, 0).reshape(NZ, 2, 32, DH)
            pj_f[i] = part
            pj_b[h, i] = part.astype(BF16)
        send(pj_b.at[h, :, :, 1 - c], pp_recv.at[h], pp_s.at[h], pp_r.at[h], partner)

    def proj_y(h):
        arrived(pp_recv.at[h], pp_s.at[h], pp_r.at[h], partner)
        for i in range(NY):
            both = pj_f[i, :, c] + pp_recv[h, i].astype(F32)
            py_send[h, i] = both.astype(BF16)
        py_own[...] = pj_f[y, :, c] + pp_recv[h, y].astype(F32)
        for d in (1, -1, 2):
            send(py_send.at[h, yat(d)], py_recv.at[h, d % 4], py_s.at[h, d % 4], py_r.at[h, d % 4], ydev[d])

    def proj_z(h):
        total = py_own[...]
        for d in (1, -1, 2):
            arrived(py_recv.at[h, d % 4], py_s.at[h, d % 4], py_r.at[h, d % 4], ydev[d])
            total = total + py_recv[h, d % 4].astype(F32)
        pz_own[...] = total
        pz_send[h] = total.astype(BF16)
        for d in (1, -1, 2, -2, 3, -3, 4):
            send(pz_send.at[h, zat(d)], pz_recv.at[h, d % 8], pz_s.at[h, d % 8], pz_r.at[h, d % 8], zdev[d])

    def proj_end(h):
        total = pz_own[z]
        for d in (1, -1, 2, -2, 3, -3, 4):
            arrived(pz_recv.at[h, d % 8], pz_s.at[h, d % 8], pz_r.at[h, d % 8], zdev[d])
            total = total + pz_recv[h, d % 8].astype(F32)
        pg_ref[:, h * DH : (h + 1) * DH] = total

    def p3_pair(h, j, v, k):
        dp = mm(da_ref[h], v, 1, 1)
        w0 = s_ref[j] * stat_a[...]
        w1 = s_ref[j + 1] * stat_a[...]
        d0 = w0 * (dp[:, :128] - stat_b[...])
        d1 = w1 * (dp[:, 128:] - stat_b[...])
        ds = jnp.concatenate([d0, d1], 1).astype(BF16)
        acc_ref[...] += mm(ds, k, 1, 0)
        return w0, w1, ds

    def p3_own(h):
        acc_ref[...] = jnp.zeros((256, 128), F32)
        q = q_of(h)
        w0, w1, ds = p3_pair(h, 32, own_kv[1], own_kv[0])
        wb = jnp.concatenate([w0, w1], 1).astype(BF16)
        cg_send[h, 0] = (mm(ds, q, 0, 0) * scale).astype(BF16)
        cg_send[h, 1] = mm(wb, da_ref[h], 0, 0).astype(BF16)
        send(cg_send.at[h], cg_recv.at[h], cg_s.at[h], cg_r.at[h], before)
        w0, w1, ds = p3_pair(h, 34, own_kv[3], own_kv[2])
        wb = jnp.concatenate([w0, w1], 1).astype(BF16)
        s_ref[32] = mm(ds, q, 0, 0) * scale
        s_ref[33] = mm(wb, da_ref[h], 0, 0)

    def p3(h, lo, hi):
        def step(i, carry):
            p3_pair(h, i * 2, pair(kvs[h], i * 2, 1), pair(kvs[h], i * 2, 0))
            return carry

        lax.fori_loop(lo, hi, step, 0)

    def p3_end(h):
        cols = slice(h * DH, (h + 1) * DH)
        qg_ref[:, cols] = (acc_ref[...] * scale).astype(BF16)
        arrived(cg_recv.at[h], cg_s.at[h], cg_r.at[h], after)
        kg_ref[:, cols] = (s_ref[32] + cg_recv[h, 0].astype(F32)).astype(BF16)
        vg_ref[:, cols] = (s_ref[33] + cg_recv[h, 1].astype(F32)).astype(BF16)

    def layer(h_wait=range(HD)):
        w_wait()
        total = jnp.zeros((256, 512), F32)
        for h in range(HD):
            total = total + mm(at_own[h], w_col[x, h * DH : (h + 1) * DH], 1, 0)
        for d in (1, -1, 2):
            peer = xat(-d)
            for h in range(HD):
                arrived(at_all.at[peer, h], at_s.at[h, d % 4], at_r.at[h, d % 4], xdev[d])
                total = total + mm(at_all[peer, h], w_col[peer, h * DH : (h + 1) * DH], 1, 0)
        lo_ref[...] = total.astype(BF16)

    half = R // 4
    full = R // 2

    def unit(h, u):
        if u == 0:
            p1_own(h)
            p1(h, 0, full)
        elif u == 1:
            p2_own(h)
            p2(h, 0, full)
            finish_fwd(h)
            proj(h)
        elif u == 2:
            p3_own(h)
            proj_y(h)
            p3(h, 0, half)
        elif u == 3:
            proj_z(h)
            p3(h, half, full)
            p3_end(h)

    slot_ticks(0)
    x_sends()
    last = STAGGER * (HD - 1) + 7
    for t in range(1, last + 1):
        if t == 5:
            og_wait()
            make_da()
        slot_ticks(t)
        for h in range(HD - 1):
            u = t - STAGGER * h - 7
            if 0 <= u < 4:
                if u == 0 and h > 0:
                    proj_end(h - 1)
                unit(h, u)
    h = HD - 1
    proj_end(h - 1)
    for u in range(4):
        unit(h, u)
    layer()
    proj_end(h)
    for cp in sent:
        cp.wait_send()


def per_device(queries, keys, values, out_grad, out_weight, retr_owner, retr_block):
    vm = pl.BlockSpec(memory_space=pltpu.VMEM)
    hbm = pl.BlockSpec(memory_space=pl.ANY)
    sm = pl.BlockSpec(memory_space=pltpu.SMEM)
    dma = pltpu.SemaphoreType.DMA
    block16 = jax.ShapeDtypeStruct((256, 512), BF16)
    kv_shape = pltpu.VMEM((NY, NZ, 2, 4, 128, DH), BF16)
    return pl.pallas_call(
        body,
        name="memory_attention",
        out_shape=(block16, block16, block16, block16, jax.ShapeDtypeStruct((32, 512), F32)),
        in_specs=[vm, hbm, hbm, vm, vm, sm, sm],
        out_specs=(vm, vm, vm, vm, vm),
        scratch_shapes=[
            kv_shape, kv_shape, kv_shape, kv_shape,
            pltpu.VMEM((36, 256, 128), F32),
            pltpu.VMEM((256, 128), F32),
            pltpu.VMEM((256, 128), F32),
            pltpu.VMEM((256, 128), F32),
            pltpu.VMEM((NX, 256, 512), BF16),
            pltpu.VMEM((NX, 512, 256), BF16),
            pltpu.VMEM((NX, 512, 512), BF16),
            pltpu.VMEM((HD, 256, DH), BF16),
            pltpu.VMEM((HD, 256, DH), BF16),
            pltpu.VMEM((NX, HD, 256, DH), BF16),
            pltpu.VMEM((NY, NZ, 2, 32, DH), F32),
            pltpu.VMEM((HD, NY, NZ, 2, 32, DH), BF16),
            pltpu.VMEM((HD, NY, NZ, 32, DH), BF16),
            pltpu.VMEM((HD, NY, NZ, 32, DH), BF16),
            pltpu.VMEM((NZ, 32, DH), F32),
            pltpu.VMEM((HD, 4, NZ, 32, DH), BF16),
            pltpu.VMEM((HD, NZ, 32, DH), BF16),
            pltpu.VMEM((NZ, 32, DH), F32),
            pltpu.VMEM((HD, NZ, 32, DH), BF16),
            pltpu.VMEM((HD, 2, 256, DH), BF16),
            pltpu.VMEM((HD, 2, 256, DH), BF16),
            pltpu.VMEM((4, 256, DH), BF16),
            dma((5, 4)),
            dma((HD, 2, 4)), dma((HD, 2, 4)),
            dma((HD, 2, 4)), dma((HD, 2, 4)),
            dma((HD, 2, 2)), dma((HD, 2, 2)),
            dma((HD, 2, 8)), dma((HD, 2, 8)),
            dma((HD, 8)), dma((HD, 8)),
            dma((HD, 8)), dma((HD, 8)),
            dma((HD, 8)), dma((HD, 8)),
            dma((4,)), dma((4,)),
            dma((4,)), dma((4,)),
            dma((HD, 4)), dma((HD, 4)),
            dma((HD,)), dma((HD,)),
            dma((HD, 4)), dma((HD, 4)),
            dma((HD, 8)), dma((HD, 8)),
            dma((HD,)), dma((HD,)),
        ],
        compiler_params=pltpu.CompilerParams(
            collective_id=0, has_side_effects=True, vmem_limit_bytes=66 * 1024 * 1024 - 2**21 - 2**20
        ),
    )(queries, keys, values, out_grad, out_weight, retr_owner, retr_block)


def solution(mesh):
    spec = P("seg", "head")
    return jax.shard_map(
        per_device,
        mesh=mesh,
        in_specs=(spec, spec, spec, spec, P("head", None), P(), P()),
        out_specs=(spec,) * 5,
        check_vma=False,
    )
```
